32 devices in a mesh: dp: 16 (over z, x, core), opt: 2 (over y).
Axes of the slice: x: 2, y: 2, z: 4, core: 2. Of those that a mesh axis runs over, the one named last changes fastest.
Arguments:
- params: bfloat16 [12595200], P('opt'), may hold values from -2 to 2, as said below
- moment_one: float32 [12595200], P('opt'), may hold values from -160 to 160
- moment_two: float32 [12595200], P('opt'), may hold values from 81.92 to 8192
- inputs: bfloat16 [64, 128, 1024], P(('dp', 'opt')), may hold values from -6 to 6
- cotangent: bfloat16 [64, 128, 1024], P(('dp', 'opt')), may hold values from -6 to 6
- segments: int32 [64, 128], P(('dp', 'opt')), may hold values from 0 to 3, never falling along the last dimension, each value on 1 to 64 neighbouring positions
- windows: int32 [64], P(('dp', 'opt')), may hold values from 128 to 512, as said below
Outputs:
- output: bfloat16 [64, 128, 1024], P(('dp', 'opt'))
- input_grad: bfloat16 [64, 128, 1024], P(('dp', 'opt'))
- grads: float32 [12595200], P('opt')
- new_params: float32 [12595200], P('opt')
- new_moment_one: float32 [12595200], P('opt')
- new_moment_two: float32 [12595200], P('opt')
- new_copy: bfloat16 [12595200], P('opt')
The draws below stay inside these ranges and needn't reach their ends.
Inputs may be any that keep to these rules, and one draw needn't show every extreme that they name: `params`: the flat parameter vector in the layout of the steps; gains near 1. `windows`: every draw holds a sequence with window 512 and one with window 512 // 4.
All inputs are finite; a program needn't handle non-finite values.
Results may differ from the reference program's by a relative error of at most 0.0094.
Values may be sent and summed in bfloat16 or wider, within the bound.
No kernel may reach another device: no remote copies, remote signals or barrier semaphores. Data moves between devices by JAX's collectives and lax.ppermute only.
A program may use at most 448 MiB of HBM per device.

```python
import math
import jax
import jax.numpy as jnp
import numpy as np
from jax import lax

D = 1024
HEADS = 16
HEAD_DIM = 64
FF = 4096
SEQ_LEN = 128
MICRO = 2
WINDOW = 512
SEQS = 64
TOKENS = 8192
MATRIX_PARAMS = 12582912
PARAMS = 12595200


def scaled_noise(key, amount, scale_value):
    return jnp.clip(jax.random.normal(key, (amount,), jnp.float32), -6.0, 6.0) * scale_value


def draw_params(key, part):
    keys_list = jax.random.split(key, 13)
    pieces = [scaled_noise(keys_list[0], D * 3 * D, 1.0 / math.sqrt(D)), scaled_noise(keys_list[1], D * D, 4.0 / math.sqrt(D)), scaled_noise(keys_list[2], D * FF, 1.0 / math.sqrt(D)), scaled_noise(keys_list[3], FF * D, 1.5 / math.sqrt(FF)), 1.0 + scaled_noise(keys_list[4], D, 0.12), scaled_noise(keys_list[5], D, 0.3), scaled_noise(keys_list[6], D, 0.3), scaled_noise(keys_list[7], D, 0.3), scaled_noise(keys_list[8], D, 0.3), 1.0 + scaled_noise(keys_list[9], D, 0.12), scaled_noise(keys_list[10], D, 0.3), scaled_noise(keys_list[11], FF, 0.3), scaled_noise(keys_list[12], D, 0.3)]
    return jnp.clip(jnp.concatenate(pieces), -2.0, 2.0).astype(jnp.bfloat16)


def draw_windows(key, part):
    drawn = jax.random.randint(key, (SEQS,), WINDOW // 4, WINDOW + 1, dtype=jnp.int32)
    return drawn.at[0].set(WINDOW).at[1].set(WINDOW // 4)


def block_levels(own_key, dims, cuts, least, high):
    def one(dim, parts):
        heights = jax.random.uniform(jax.random.fold_in(jax.random.fold_in(own_key, 6), dim), (parts,), jnp.float32, least / len(cuts), high / len(cuts))
        return jnp.repeat(jnp.exp(heights), dims[dim] // parts).reshape((-1,) + (1,) * (len(dims) - dim - 1))

    loudness = one(*cuts[0])
    for cut in cuts[1:]:
        loudness = loudness * one(*cut)
    return loudness


def split_up(number_of, total, most, skew):
    loads = [(1 << 20) // math.isqrt(standing ** skew) + 1 for standing in range(2, number_of + 1)]
    rest, holding = total - most - (number_of - 1), [1] * (number_of - 1)
    while rest > 0:
        movable = [i for i in range(number_of - 1) if holding[i] < most]
        whole, budget = sum([loads[i] for i in movable]), rest
        for i in movable:
            extra = min(most - holding[i], max(1, budget * loads[i] // whole), rest)
            holding[i] = holding[i] + extra
            rest = rest - extra
    return np.array([most] + holding)


def uneven_parts(key, count, total, limit, lean):
    if count == 2:
        one = jax.random.randint(key, (), max(1, total - limit), min(limit, total - 1) + 1)
        return jnp.stack([one, total - one])
    lengths = jnp.asarray(split_up(count, total, limit, lean), jnp.int32)
    twos = (count - 1) // 2
    donor, taker = lengths[1:1 + 2 * twos:2], lengths[2:2 + 2 * twos:2]
    room = jnp.minimum(donor - 1, limit - taker)
    passed = jax.random.randint(jax.random.fold_in(key, 1), (twos,), 0, 1 << 20) % (room + 1)
    lengths = lengths.at[1:1 + 2 * twos:2].set(donor - passed).at[2:2 + 2 * twos:2].set(taker + passed)
    return lengths[jax.random.permutation(jax.random.fold_in(key, 2), count)]


def gaussian(own_key, shape, deviation, most, cuts=(), kind=jnp.bfloat16):
    values = jax.random.normal(own_key, shape, jnp.float32) * deviation
    if len(cuts) > 0:
        values = block_levels(own_key, shape, cuts, -0.22, 0.18) * values
    return jnp.clip(values, min=-most, max=most).astype(kind)


def setup_inputs(seed: int = 0) -> dict:
    splits = jax.random.split(jax.random.key(seed), 8)
    params = draw_params(jax.random.fold_in(splits[7], 71), 0)
    moment_one = gaussian(splits[1], (PARAMS,), (0.3 * TOKENS ** 0.5), 160.0, ((0, 2),), jnp.float32)
    moment_two = jnp.clip(jnp.exp(math.log(8192.0) - 4.6051702 * jax.random.uniform(splits[2], (PARAMS,), jnp.float32) ** block_levels(splits[2], (PARAMS,), ((0, 2),), -0.2, 0.2)), 81.92, 8192.0)
    inputs = gaussian(splits[3], (SEQS, SEQ_LEN, D), 1.0, 6.0, ((0, 32),))
    cotangent = gaussian(splits[4], (SEQS, SEQ_LEN, D), 1.0, 6.0, ((0, 32),))
    segments = jax.vmap(lambda own: jnp.searchsorted(jnp.cumsum(uneven_parts(own, 4, SEQ_LEN, SEQ_LEN // 2, 0)), jnp.arange(SEQ_LEN), side="right"))(jax.random.split(splits[5], SEQS)).reshape((SEQS, SEQ_LEN)).astype(jnp.int32)
    windows = draw_windows(jax.random.fold_in(splits[7], 71), 0)
    return {"params": params, "moment_one": moment_one, "moment_two": moment_two, "inputs": inputs, "cotangent": cotangent, "segments": segments, "windows": windows}


@jax.custom_vjp
def low(v):
    return lax.optimization_barrier(v.astype(jnp.bfloat16)).astype(jnp.float32)

@jax.custom_vjp
def low_back(v):
    return v

def low_keep(v):
    return (low(v), None)

def low_pass(kept, grad):
    return (grad,)

def back_keep(v):
    return (v, None)

def back_low(kept, grad):
    return (low(grad),)
low.defvjp(low_keep, low_pass)
low_back.defvjp(back_keep, back_low)
HIGH = lax.Precision.HIGHEST
GELU_C = math.sqrt(2.0 / math.pi)
LEARN_RATE = 0.01
WEIGHT_DECAY = 0.1

def unpack_weights(flat_values):
    layout = [(D, 3 * D), (D, D), (D, FF), (FF, D)] + [(D,)] * 7 + [(FF,), (D,)]
    pieces = []
    position = 0
    for piece_dims in layout:
        amount = math.prod(piece_dims)
        pieces.append(flat_values[position:position + amount].reshape(piece_dims))
        position = position + amount
    return pieces

def normalize(values, gain, shift_vec):
    centred = values - lax.optimization_barrier(jnp.mean(values, axis=-1, keepdims=True))
    variance = lax.optimization_barrier(jnp.mean(centred * centred, axis=-1, keepdims=True))
    return centred * lax.rsqrt(variance + 1e-05) * gain + shift_vec

def gelu_value(values):
    return 0.5 * values * (1.0 + jnp.tanh(GELU_C * (values + 0.044715 * values * values * values)))

def attend(packed):
    queries, keys_all, values_all, segment_ids, window_len = packed
    query_heads = queries.reshape(SEQ_LEN, HEADS, HEAD_DIM)
    key_heads = keys_all.reshape(SEQ_LEN, HEADS, HEAD_DIM)
    value_heads = values_all.reshape(SEQ_LEN, HEADS, HEAD_DIM)
    scores = low_back(jnp.einsum('qhd,khd->hqk', query_heads, key_heads, precision=HIGH) * (1.0 / math.sqrt(HEAD_DIM)))
    positions = jnp.arange(SEQ_LEN)
    allowed = (positions[None, :] <= positions[:, None]) & (positions[:, None] - positions[None, :] < window_len) & (segment_ids[:, None] == segment_ids[None, :])
    masked = jnp.where(allowed[None], scores, -jnp.inf)
    log_total = jax.nn.logsumexp(masked, axis=-1, keepdims=True)
    probs = low(jnp.exp(masked - log_total))
    mixed = jnp.einsum('hqk,khd->qhd', probs, value_heads, precision=HIGH)
    return mixed.reshape(SEQ_LEN, D)

def forward(flat_values, input_values, segment_part, window_part):
    qkv_weight, out_weight, fc_weight, proj_weight, first_gain, first_shift, query_bias, value_bias, out_bias, second_gain, second_shift, fc_bias, proj_bias = unpack_weights(flat_values)
    residual_in = input_values.reshape(-1, D)
    hidden_one = low(normalize(residual_in, first_gain, first_shift))
    qkv_bias = jnp.concatenate([query_bias, jnp.zeros_like(query_bias), value_bias])
    projected = low(low_back(jnp.dot(hidden_one, qkv_weight, precision=HIGH) + qkv_bias))
    projected = projected.reshape(MICRO, SEQ_LEN, 3 * D)
    mixed = lax.map(jax.checkpoint(attend), (projected[:, :, :D], projected[:, :, D:2 * D], projected[:, :, 2 * D:], segment_part, window_part))
    mixed = low(low_back(mixed.reshape(-1, D)))
    attended = low_back(jnp.dot(mixed, out_weight, precision=HIGH) + out_bias)
    residual_mid = residual_in + attended
    hidden_two = low(normalize(residual_mid, second_gain, second_shift))
    before_act = low_back(jnp.dot(hidden_two, fc_weight, precision=HIGH) + fc_bias)
    activated = low(gelu_value(before_act))
    result = residual_mid + jnp.dot(activated, proj_weight, precision=HIGH) + proj_bias
    return result.reshape(input_values.shape)

def reference(params, moment_one, moment_two, inputs, cotangent, segments, windows):
    flat_values = params.astype(jnp.float32)
    group_count = SEQS // MICRO
    input_groups = inputs.reshape(group_count, MICRO, SEQ_LEN, D)
    cot_groups = cotangent.reshape(group_count, MICRO, SEQ_LEN, D)
    segment_groups = segments.reshape(group_count, MICRO, SEQ_LEN)
    window_groups = windows.reshape(group_count, MICRO)

    def group_step(grad_total, pieces):
        input_part, cot_part, segment_part, window_part = pieces

        def forward_part(flat_part, input_values):
            return forward(flat_part, input_values, segment_part, window_part)
        out_values, pullback = jax.vjp(forward_part, flat_values, input_part.astype(jnp.float32))
        grad_flat, grad_inputs = pullback(cot_part.astype(jnp.float32))
        return (grad_total + grad_flat, (out_values.astype(jnp.bfloat16), grad_inputs.astype(jnp.bfloat16)))
    grad_total, (outputs, input_grads) = lax.scan(group_step, jnp.zeros((PARAMS,), jnp.float32), (input_groups, cot_groups, segment_groups, window_groups))
    first_moment = 0.5 * moment_one + 0.5 * grad_total
    second_moment = 0.5 * moment_two + 0.5 * grad_total * grad_total
    decay_mask = (jnp.arange(PARAMS) < MATRIX_PARAMS).astype(jnp.float32)
    update = first_moment / (jnp.sqrt(second_moment) + 1e-08) + WEIGHT_DECAY * decay_mask * flat_values
    new_values = flat_values - LEARN_RATE * update
    return (outputs.reshape(SEQS, SEQ_LEN, D), input_grads.reshape(SEQS, SEQ_LEN, D), grad_total, new_values, first_moment, second_moment, new_values.astype(jnp.bfloat16))
```

```python
import functools
import math

import jax
import jax.numpy as jnp
import numpy as np
from jax import lax
from jax.experimental import pallas as pl
from jax.experimental.pallas import tpu as pltpu
from jax.sharding import PartitionSpec as P

HEADS = 16
HEAD_DIM = 64
FF = 4096
MATRIX_PARAMS = 12582912

GELU_C = math.sqrt(2.0 / math.pi)
LEARN_RATE = 0.01
WEIGHT_DECAY = 0.1
LANES = 128
ROUNDS = 3
POST_ORDER = (1, 0, 2, 0, 1, 0, 2, 0, 1, 0, 2, 1, 0, 2, 1, 0, 2, 1, 2, 1, 2, 1, 2, 1, 2)
BF = jnp.bfloat16
F32 = jnp.float32


def layout_of(model_width, hidden_units):
    layout = [
        (model_width, 3 * model_width),
        (model_width, model_width),
        (model_width, hidden_units),
        (hidden_units, model_width),
    ]
    return layout + [(model_width,)] * 7 + [(hidden_units,), (model_width,)]


def standardize(values):
    centred = values - jnp.mean(values, axis=-1, keepdims=True)
    inverse = lax.rsqrt(jnp.mean(centred * centred, axis=-1, keepdims=True) + 1e-05)
    return (centred * inverse, inverse)


def norm_back(grad_norm, normed, inverse):
    return inverse * (
        grad_norm
        - jnp.mean(grad_norm, axis=-1, keepdims=True)
        - normed * jnp.mean(grad_norm * normed, axis=-1, keepdims=True)
    )


def dot(a, b):
    return jnp.dot(a, b, preferred_element_type=F32)


def dot_t(a, b):
    return lax.dot_general(a, b, (((1,), (1,)), ((), ())), preferred_element_type=F32)


def compute(
    matrix, advance, vectors, inputs, cotangent, segments, windows, buffers, starts, line, turn_of
):
    (
        first_gain, first_shift, query_bias, value_bias, out_bias,
        second_gain, second_shift, fc_bias, proj_bias,
    ) = vectors
    qkv_weight = matrix(0)
    micro, seq_rows, width = inputs.shape
    rows = micro * seq_rows
    scale = 1.0 / math.sqrt(HEAD_DIM)
    first_gain_f = first_gain.astype(F32)
    second_gain_f = second_gain.astype(F32)
    residual_in = inputs.reshape(rows, width).astype(F32)
    dy = cotangent.reshape(rows, width)
    normed_one, inverse_one = standardize(residual_in)
    hidden_one = (normed_one * first_gain_f + first_shift.astype(F32)).astype(BF)
    qkv_bias = jnp.concatenate([query_bias, jnp.zeros_like(query_bias), value_bias]).astype(F32)
    projected = (dot(hidden_one, qkv_weight) + qkv_bias).astype(BF)
    advance(2)
    split = lambda v: v.reshape(micro, seq_rows, HEADS, HEAD_DIM)
    queries = split(projected[:, :width])
    keys = split(projected[:, width : 2 * width])
    values = split(projected[:, 2 * width :])
    pos = jnp.arange(seq_rows)
    gap = pos[:, None] - pos[None, :]
    allowed = (
        (gap >= 0)[None]
        & (gap[None] < windows[:, None, None])
        & (segments[:, :, None] == segments[:, None, :])
    )[:, None]
    scores = jnp.einsum("bqhd,bkhd->bhqk", queries, keys, preferred_element_type=F32) * scale
    scores = jnp.where(allowed, scores, -jnp.inf)
    row_max = jnp.max(scores, axis=-1, keepdims=True)
    log_total = row_max + jnp.log(jnp.sum(jnp.exp(scores - row_max), axis=-1, keepdims=True))
    exact = jnp.exp(scores - log_total)
    probs = exact.astype(BF)
    mixed = jnp.einsum("bhqk,bkhd->bqhd", probs, values, preferred_element_type=F32)
    mixed = mixed.reshape(rows, width).astype(BF)
    out_weight = matrix(1)
    residual_mid = residual_in + (dot(mixed, out_weight) + out_bias.astype(F32))
    normed_two, inverse_two = standardize(residual_mid)
    hidden_two = (normed_two * second_gain_f + second_shift.astype(F32)).astype(BF)
    fc_weight = matrix(2)
    before = dot(hidden_two, fc_weight) + fc_bias.astype(F32)
    tangent = jnp.tanh(GELU_C * (before + 0.044715 * before * before * before))
    act = (0.5 * before * (1.0 + tangent)).astype(BF)
    slope = 0.5 * (1.0 + tangent) + 0.5 * before * (1.0 - tangent * tangent) * GELU_C * (
        1.0 + 0.134145 * before * before
    )
    proj_weight = matrix(3)
    output = (residual_mid + (dot(act, proj_weight) + proj_bias.astype(F32))).astype(BF)
    buffers.matrix(starts[3], act, dy)
    grad_before = (dot_t(dy, proj_weight) * slope).astype(BF)
    buffers.matrix(starts[2], hidden_two, grad_before)
    turn_of(0)
    grad_hidden_two = dot_t(grad_before, fc_weight)
    grad_mid = dy.astype(F32) + norm_back(grad_hidden_two * second_gain_f, normed_two, inverse_two)
    grad_attended = grad_mid.astype(BF)
    turn_of(0)
    (grad_attended,) = line.through([grad_attended])
    buffers.matrix(starts[1], mixed, grad_attended)
    grad_mixed = split(dot_t(grad_attended, out_weight).astype(BF))
    grad_probs = jnp.einsum("bqhd,bkhd->bhqk", grad_mixed, values, preferred_element_type=F32)
    row_terms = jnp.sum(exact * grad_probs, axis=-1, keepdims=True)
    grad_scores = (exact * (grad_probs - row_terms)).astype(BF)
    grad_q = jnp.einsum("bhqk,bkhd->bqhd", grad_scores, keys, preferred_element_type=F32) * scale
    grad_k = jnp.einsum("bhqk,bqhd->bkhd", grad_scores, queries, preferred_element_type=F32) * scale
    grad_v = jnp.einsum("bhqk,bqhd->bkhd", probs, grad_mixed, preferred_element_type=F32)
    grad_projected = jnp.concatenate(
        [g.reshape(rows, width).astype(BF) for g in (grad_q, grad_k, grad_v)], axis=1
    )
    turn_of(0)
    buffers.matrix(starts[0], hidden_one, grad_projected)
    turn_of(1)
    turn_of(0)
    grad_hidden_one = dot_t(grad_projected, qkv_weight)
    grad_input = (
        grad_mid + norm_back(grad_hidden_one * first_gain_f, normed_one, inverse_one)
    ).astype(BF)
    column = lambda v: jnp.sum(v.astype(F32), axis=0)
    qkv_columns = column(grad_projected)
    grads = [
        column(grad_hidden_one * normed_one), column(grad_hidden_one),
        qkv_columns[:width], qkv_columns[2 * width :], column(grad_attended),
        column(grad_hidden_two * normed_two), column(grad_hidden_two),
        column(grad_before), column(dy),
    ]
    buffers.vectors(
        starts[4], jnp.concatenate([v.astype(BF).reshape(-1, LANES) for v in grads])
    )
    turn_of(2)
    return output.reshape(inputs.shape), grad_input.reshape(inputs.shape)


def bits_of(count):
    return count.bit_length() - 1


def xor_permute(value, bit, count, axis):
    return lax.ppermute(value, axis, [(i, i ^ (1 << bit)) for i in range(count)])


def halving_orders(opt_bits, dp_bits):
    opts = [("opt", b) for b in range(opt_bits)]
    core, *others = [("dp", b) for b in range(dp_bits)]
    return ([core, *others[:1], *opts, *others[1:]], [core, *opts, *others])


class Line:
    def __init__(self):
        self.token = jnp.zeros((8, LANES), F32)

    def call(self, kernel, args, outs, in_specs, out_specs, name, grid=(), prefetch=0, scratch=(), aliases=None):
        token = pl.BlockSpec(memory_space=pl.ANY)
        n_in, n_out = len(in_specs) + prefetch, len(outs)

        def chained(*refs):
            rest = refs[n_in + 1 :]
            kernel(*refs[:n_in], *rest[:n_out], *rest[n_out + 1 :])

        *results, self.token = pl.pallas_call(
            chained,
            out_shape=[*outs, jax.ShapeDtypeStruct((8, LANES), F32)],
            grid_spec=pltpu.PrefetchScalarGridSpec(
                num_scalar_prefetch=prefetch,
                grid=grid,
                in_specs=[*in_specs, token],
                out_specs=[*out_specs, token],
                scratch_shapes=list(scratch),
            ),
            input_output_aliases=aliases or {},
            name=name,
        )(*args, self.token)
        return results


    def through(self, values):
        spec = pl.BlockSpec(memory_space=pl.ANY)
        return self.call(
            lambda *refs: None,
            values,
            [jax.ShapeDtypeStruct(v.shape, v.dtype) for v in values],
            [spec] * len(values),
            [spec] * len(values),
            "through",
            aliases={n: n for n in range(len(values))},
        )


ANYWHERE = pl.BlockSpec(memory_space=pl.ANY)
IN_VMEM = pl.BlockSpec(memory_space=pltpu.VMEM)


def combine_kernel(groups, joined, count, rows, table_ref, *refs):
    n_in = sum(groups)
    n_out = 1 if joined else len(groups)
    arrays, outs, held, sem = refs[:n_in], refs[n_in : n_in + n_out], refs[-2], refs[-1]
    plain = n_in == 1

    def copy(n, i):
        source = arrays[n].at[pl.ds(pl.multiple_of(table_ref[n * count + i] * rows, 8), rows), :]
        target = outs[0] if plain else held.at[n]
        return pltpu.make_async_copy(source, target.at[pl.ds(i * rows, rows), :], sem)

    for n in range(n_in):
        for i in range(count):
            copy(n, i).start()
    for n in range(n_in):
        whole = outs[0] if plain else held.at[n]
        pltpu.make_async_copy(whole, whole, sem).wait()
    if plain:
        return
    for i in range(count):
        at = 0
        for g, size in enumerate(groups):
            total = held[at, i * rows : (i + 1) * rows, :].astype(F32)
            for n in range(at + 1, at + size):
                total = total + held[n, i * rows : (i + 1) * rows, :].astype(F32)
            at += size
            if joined:
                row = (i * len(groups) + g) * rows
                outs[0][row : row + rows, :] = total.astype(BF)
            else:
                outs[g][i * rows : (i + 1) * rows, :] = total.astype(BF)


def combine(line, groups, table, count, rows, joined):
    arrays = [a for group in groups for a in group]
    shape = jax.ShapeDtypeStruct((count * rows * (len(groups) if joined else 1), LANES), BF)
    n_out = 1 if joined else len(groups)
    held = (len(arrays), count * rows, LANES) if len(arrays) > 1 else (8, LANES)
    return line.call(
        functools.partial(combine_kernel, [len(g) for g in groups], joined, count, rows),
        (table, *arrays),
        [shape] * n_out,
        [ANYWHERE] * len(arrays),
        [IN_VMEM] * n_out,
        "combine",
        prefetch=1,
        scratch=[pltpu.VMEM(held, BF), pltpu.SemaphoreType.DMA],
    )


class Halving:
    def __init__(self, line, blocks, orders, dp_count, opt_count):
        self.line = line
        self.orders, self.dp_count, self.opt_count = orders, dp_count, opt_count
        self.opt_bits, self.axes = bits_of(opt_count), bits_of(opt_count) + bits_of(dp_count)
        self.split = len(orders)
        self.rows = blocks.shape[0] // (opt_count * dp_count) // self.split
        self.terms = [[(blocks, list(range(self.axes)), True)] for _ in orders]
        self.passed = [[] for _ in orders]
        self.steps = len(orders[0])

    def axis_of(self, step):
        name, bit = step
        return self.opt_bits - 1 - bit if name == "opt" else self.axes - 1 - bit

    def bits(self):
        values = []
        for a in range(self.axes):
            name, bit = ("opt", self.opt_bits - 1 - a) if a < self.opt_bits else ("dp", self.axes - 1 - a)
            values.append((lax.axis_index(name) >> bit) & 1)
        return values

    def sums(self, n):
        step_axes = [None if n is None else self.axis_of(o[n]) for o in self.orders]
        same = set(self.passed[0]) == set(self.passed[-1]) and step_axes[0] == step_axes[-1]
        whole = self.split == 1 or (same and not self.passed[0])
        bits, tables, groups = self.bits(), [], []
        for half in range(1 if whole else self.split):
            free = [a for a in range(self.axes) if a not in self.passed[half] and a != step_axes[half]]
            count = 1 << len(free)
            numbers = np.arange(count)
            group = []
            for array, axes, both in self.terms[half]:
                row, scale = 0, 1
                for a in reversed(axes):
                    if a in free:
                        row = row + scale * ((numbers >> (len(free) - 1 - free.index(a))) & 1)
                    else:
                        row = row + scale * (1 - bits[a] if a == step_axes[half] else bits[a])
                    scale *= 2
                if both and not whole:
                    row = row * self.split + half
                tables.append(jnp.broadcast_to(row, (count,)))
                group.append(array)
            groups.append(group)
        table = jnp.concatenate(tables).astype(jnp.int32)
        rows = self.rows * self.split if whole else self.rows
        self.same = same
        return combine(self.line, groups, table, count, rows, same)

    def exchange(self, n, sends):
        recvs = []
        for half, send in enumerate(sends):
            name, bit = self.orders[half][n]
            recvs.append(xor_permute(send, bit, self.opt_count if name == "opt" else self.dp_count, name))
        return recvs

    def incoming(self, n, recvs):
        for half, order in enumerate(self.orders):
            self.passed[half].append(self.axis_of(order[n]))
            left = [a for a in range(self.axes) if a not in self.passed[half]]
            self.terms[half].append((recvs[0 if self.same else half], left, self.same))


def join_kernel(left_ref, right_ref, out_ref):
    rows = left_ref.shape[0]
    out_ref[:rows, :] = left_ref[...]
    out_ref[rows:, :] = right_ref[...]


def join(line, left, right):
    shape = jax.ShapeDtypeStruct((2 * left.shape[0], LANES), BF)
    return line.call(join_kernel, (left, right), [shape], [IN_VMEM] * 2, [IN_VMEM], "join")[0]


class Spread:
    def __init__(self, line, value, group, dp_count):
        self.line = line
        self.near, self.dp_count = [value], dp_count
        self.bits = list(range(bits_of(group) - 1, -1, -1))
        self.far = None

    def outgoing(self):
        if len(self.near) == 2 and self.bits[0]:
            self.near = [join(self.line, *self.near)]
        elif len(self.near) == 2:
            self.near = self.line.through(self.near)
        return self.near

    def exchange(self, sends):
        self.near = sends
        return [xor_permute(v, self.bits[0], self.dp_count, "dp") for v in sends]

    def incoming(self, recvs):
        if self.bits.pop(0):
            self.near = [*self.near, *recvs]
        else:
            self.far = recvs


def spread_place(relative, group):
    bits = bits_of(group)
    return sum(((relative >> (bits - 1 - i)) & 1) << i for i in range(bits))


def exchange_shards(value, opt_count):
    if opt_count == 2:
        return xor_permute(value, 0, opt_count, "opt")
    rows = value.shape[0]
    for bit in range(bits_of(opt_count)):
        value = jnp.concatenate([value, xor_permute(value, bit, opt_count, "opt")])
    return value[rows:]


def unflatten_kernel(plan, dims, me_ref, own_ref, *rest):
    pieces_ref, out_ref, flat, wide, sem = rest[:-4], rest[-4], rest[-3], rest[-2], rest[-1]
    height, width = dims
    across = width // LANES
    opt_me, dp_me = me_ref[0], me_ref[1]
    i = pl.program_id(0)
    shard_rows, main_rows, chunk_list, opt_count, needed, first, last = plan

    def fetch(source, at, to, count):
        pltpu.make_async_copy(
            source.at[pl.ds(pl.multiple_of(at, 8), count), :], flat.at[pl.ds(to, count), :], sem
        ).start()

    begins, begin = {}, 0
    for c in needed:
        begins[c] = begin
        begin += min(chunk_list[c][1], 4)

    @pl.when(i == 0)
    def _():
        for s in range(opt_count):
            low, high = max(first, s * shard_rows), min(last, (s + 1) * shard_rows)
            if low >= high:
                continue
            lo, hi = low - s * shard_rows, high - s * shard_rows

            @pl.when(opt_me == s)
            def _():
                fetch(own_ref, lo, low - first, high - low)

            @pl.when(opt_me != s)
            def _():
                away = (opt_me ^ s) - 1
                at = 0
                for c, (piece, group) in enumerate(chunk_list):
                    for p in range(group):
                        a, b = max(lo, at), min(hi, at + piece)
                        if a < b:
                            place = spread_place((dp_me ^ p) & (group - 1), group)
                            parts = min(group, 4)
                            each = group // parts
                            row = ((place % each) * (opt_count - 1) + away) * piece + (a - at)
                            to = a + s * shard_rows - first
                            for part in range(parts):

                                @pl.when(place // each == part)
                                def _():
                                    fetch(pieces_ref[begins[c] + part], row, to, b - a)

                        at += piece
                a = max(lo, at)
                if a < hi:
                    tail = shard_rows - main_rows
                    fetch(pieces_ref[-1], away * tail + (a - at), a + s * shard_rows - first, hi - a)
        pltpu.make_async_copy(flat, flat, sem).wait()

    step = out_ref.shape[0]
    rows = flat[pl.ds(pl.multiple_of(i * step * across, 8), step * across), :].astype(F32)
    if across % 32 == 0:
        out_ref[...] = rows.reshape(step, across, LANES).reshape(step, width).astype(BF)
    else:
        wide[...] = rows
        for j in range(across):
            out_ref[:, j * LANES : (j + 1) * LANES] = wide[pl.ds(j, step, stride=across), :].astype(BF)


def unflatten(line, own, chunks, tail, first, dims, plan, me):
    height, width = dims
    rows = height * width // LANES
    step = 256 if width <= 1024 else 64 if width <= 3072 else 128
    received = [v for chunk in chunks.values() for v in (*chunk.near, *chunk.far)]
    return line.call(
        functools.partial(unflatten_kernel, (*plan, tuple(chunks), first, first + rows), dims),
        (me, own, *received, tail),
        [jax.ShapeDtypeStruct(dims, BF)],
        [ANYWHERE] * (2 + len(received)),
        [pl.BlockSpec((step, width), lambda i, me: (i, 0))],
        "unflatten",
        grid=(height // step,),
        prefetch=1,
        scratch=[
            pltpu.VMEM((rows, LANES), BF),
            pltpu.VMEM((step * width // LANES, LANES), F32),
            pltpu.SemaphoreType.DMA,
        ],
    )[0]


def grad_kernel(targets, across, block, n_in, left_ref, right_ref, *rest):
    outs, (held, wide, sems) = rest[n_in:-3], rest[-3:]
    i, steps = pl.program_id(0), pl.num_programs(0)
    slot = lax.rem(i, 2)

    def drain(which):
        pltpu.make_async_copy(held.at[which], held.at[which], sems.at[which]).wait()

    @pl.when(i >= 2)
    def _():
        drain(slot)

    acc = lax.dot_general(
        left_ref[...], right_ref[...], (((0,), (0,)), ((), ())), preferred_element_type=F32
    )
    height = acc.shape[0]
    if across % 32 == 0:
        held[slot] = acc.reshape(height, across, LANES).astype(BF).reshape(block, LANES)
    else:
        for j in range(across):
            wide[pl.ds(j, height, stride=across), :] = acc[:, j * LANES : (j + 1) * LANES]
        held[slot] = wide[...].astype(BF)
    put_rows(targets, block, i, held.at[slot], outs, sems.at[slot])

    @pl.when(i == steps - 1)
    def _():
        drain(slot)

        @pl.when(steps > 1)
        def _():
            drain(1 - slot)


def put_rows(targets, block, i, held, outs, sem):
    for low, high, which, row in targets:
        whole_low, whole_high = -(-low // block), high // block
        if whole_low < whole_high:

            @pl.when((i >= whole_low) & (i < whole_high))
            def _():
                at = pl.multiple_of(row - low + i * block, 8)
                pltpu.make_async_copy(held, outs[which].at[pl.ds(at, block), :], sem).start()

        for b in sorted({low // block, (high - 1) // block}):
            if whole_low <= b < whole_high:
                continue
            a, e = max(low, b * block), min(high, (b + 1) * block)

            @pl.when(i == b)
            def _():
                pltpu.make_async_copy(
                    held.at[pl.ds(a - b * block, e - a), :],
                    outs[which].at[pl.ds(row + a - low, e - a), :],
                    sem,
                ).start()


def place_kernel(targets, n_in, rows_ref, *rest):
    outs, sem = rest[n_in:-1], rest[-1]
    put_rows(targets, rows_ref.shape[0], 0, rows_ref, outs, sem)
    pltpu.make_async_copy(rows_ref, rows_ref, sem).wait()


class RoundBuffers:
    def __init__(self, line, shard_rows, step, rounds, opt_count):
        self.line = line
        self.shard_rows, self.step, self.rounds, self.opt_count = shard_rows, step, rounds, opt_count
        self.arrays = [None] * rounds
        self.left = [
            sum(max(0, min(step, shard_rows - self.begin(k, s))) for s in range(opt_count))
            for k in range(rounds)
        ]

    def begin(self, k, s):
        return (self.rounds - 1 - k if s < self.opt_count // 2 else k) * self.step

    def targets(self, first, last):
        found = []
        for k in range(self.rounds):
            for s in range(self.opt_count):
                at = s * self.shard_rows + self.begin(k, s)
                end = min(at + self.step, (s + 1) * self.shard_rows)
                low, high = max(first, at), min(last, end)
                if low < high:
                    found.append((low - first, high - first, k, s * self.step + low - at))
        return found

    def write(self, first, rows, call):
        targets = self.targets(first, first + rows)
        for low, high, k, _ in targets:
            self.left[k] -= high - low
        used = sorted({t[2] for t in targets})
        targets = [(a, b, used.index(k), r) for a, b, k, r in targets]
        old = [k for k in used if self.arrays[k] is not None]
        shape = jax.ShapeDtypeStruct((self.opt_count * self.step, LANES), BF)
        outs = call(targets, [self.arrays[k] for k in old], [used.index(k) for k in old], [shape] * len(used))
        for k, array in zip(used, outs):
            self.arrays[k] = array

    def matrix(self, first, left, right):
        tokens, height = left.shape
        width = right.shape[1]
        across = width // LANES
        high = 512 if height > 1024 else 128 if across % 32 == 0 else 256
        block = high * across

        def call(targets, old, places, shapes):
            return self.line.call(
                functools.partial(grad_kernel, targets, across, block, len(old)),
                (left, right, *old),
                shapes,
                [
                    pl.BlockSpec((tokens, high), lambda i: (0, i)),
                    pl.BlockSpec((tokens, width), lambda i: (0, 0)),
                ]
                + [ANYWHERE] * len(old),
                [ANYWHERE] * len(shapes),
                "weight_grad",
                grid=(height // high,),
                scratch=[
                    pltpu.VMEM((2, block, LANES), BF),
                    pltpu.VMEM((block if across % 32 else 8, LANES), F32),
                    pltpu.SemaphoreType.DMA((2,)),
                ],
                aliases={2 + n: p for n, p in enumerate(places)},
            )

        self.write(first, height * across, call)

    def vectors(self, first, rows):
        def call(targets, old, places, shapes):
            return self.line.call(
                functools.partial(place_kernel, targets, len(old)),
                (rows, *old),
                shapes,
                [IN_VMEM] + [ANYWHERE] * len(old),
                [ANYWHERE] * len(shapes),
                "vector_grads",
                scratch=[pltpu.SemaphoreType.DMA],
                aliases={1 + n: p for n, p in enumerate(places)},
            )

        self.write(first, rows.shape[0], call)


def adam_kernel(table_ref, g_ref, h_ref, p_ref, m_ref, v_ref, *rest):
    grad_ref, new_ref, first_ref, second_ref, copy_ref = rest[-5:]
    i = pl.program_id(0)
    rows = g_ref.shape[0]
    grad = jnp.where(i < pl.num_programs(0) // 2, g_ref[...], h_ref[...]).astype(F32)
    old = p_ref[...].astype(F32)
    first = 0.5 * m_ref[...] + 0.5 * grad
    second = 0.5 * v_ref[...] + 0.5 * grad * grad
    row = table_ref[pl.num_programs(0)] + table_ref[i] * rows + lax.broadcasted_iota(jnp.int32, grad.shape, 0)
    decay = jnp.where(row < MATRIX_PARAMS // LANES, WEIGHT_DECAY, 0.0)
    new = old - LEARN_RATE * (first / (jnp.sqrt(second) + 1e-08) + decay * old)
    grad_ref[...] = grad
    new_ref[...] = new
    first_ref[...] = first
    second_ref[...] = second
    copy_ref[...] = new.astype(BF)


def adam(line, grads, params, first, second, blocks, offset, piece, previous):
    rows = params.shape[0]
    count = grads[0].shape[0] // piece
    moved = pl.BlockSpec((piece, LANES), lambda i, t: (t[i], 0))
    outs = [jax.ShapeDtypeStruct((rows, LANES), t) for t in (F32, F32, F32, F32, BF)]
    table = jnp.concatenate([blocks, offset.reshape(1)]).astype(jnp.int32)
    return line.call(
        adam_kernel,
        (table, *grads, params, first, second, *previous),
        outs,
        [
            pl.BlockSpec((piece, LANES), lambda i, t: (jnp.minimum(i, count - 1), 0)),
            pl.BlockSpec((piece, LANES), lambda i, t: (jnp.maximum(i - count, 0), 0)),
            moved,
            moved,
            moved,
        ]
        + [ANYWHERE] * len(previous),
        [moved] * 5,
        "adam",
        grid=(2 * count,),
        prefetch=1,
        aliases={6 + i: i for i in range(len(previous))},
    )


def gather_weights(rows, layout, opt_count, dp_count, opt_me, dp_me, line):
    shard_rows = rows.shape[0]
    starts = [0]
    for dims in layout:
        starts.append(starts[-1] + math.prod(dims) // LANES)
    vector_rows = starts[-1] - starts[4]
    unit = 8 * dp_count
    units = (shard_rows - vector_rows) // unit
    main_rows = units * unit
    half, spread_part, sixth = -(-units // 2), 3 * units // 16, units // 6
    chunk_list = [
        (8 * spread_part, dp_count),
        ((half - spread_part) * unit // 2, 2),
        (8 * (units - half - sixth), dp_count),
        (sixth * unit // 2, 2),
    ]
    owned, at = [rows[main_rows:]], 0
    for piece, group in chunk_list:
        owned.append(lax.dynamic_slice(rows, (at + (dp_me & (group - 1)) * piece, 0), (piece, LANES)))
        at += piece * group
    moving = {}
    for n in (0, 1, 3, 2):
        moving[n] = exchange_shards(owned[n], opt_count)
    tail = moving[0]
    chunks = [None] * len(chunk_list)

    def advance(n):
        spread = chunks[n]
        if spread is not None and spread.far is not None:
            return
        if spread is None:
            spread = chunks[n] = Spread(line, moving[n + 1], chunk_list[n][1], dp_count)
        else:
            spread.incoming(moving[n + 1])
        if spread.bits:
            moving[n + 1] = spread.exchange(spread.outgoing())

    for n in range(bits_of(dp_count)):
        advance(0)
        if n:
            advance(2)
        if n == 1:
            moving[4] = exchange_shards(*line.through([owned[4]]), opt_count)
    plan = (shard_rows, main_rows, chunk_list, opt_count)
    me = jnp.stack([opt_me, dp_me]).astype(jnp.int32)

    def matrix(n):
        first, last = starts[n], starts[n + 1]
        needed, at = {}, 0
        for c, (piece, group) in enumerate(chunk_list):
            end = at + piece * group
            if any(
                max(first - s * shard_rows, at) < min(last - s * shard_rows, end)
                for s in range(opt_count)
            ):
                while chunks[c] is None or chunks[c].far is None:
                    advance(c)
                needed[c] = chunks[c]
            at = end
        return unflatten(line, rows, needed, tail, first, layout[n], plan, me)

    owner = opt_count - 1
    tail_rows = shard_rows - main_rows
    stacked = jnp.concatenate([rows[main_rows:], tail])
    flat = lax.dynamic_slice(
        stacked, ((opt_me ^ owner) * tail_rows + tail_rows - vector_rows, 0), (vector_rows, LANES)
    )
    vectors = []
    for start, dims in zip(starts[4:], layout[4:]):
        at = start - starts[4]
        vectors.append(flat[at : at + dims[0] // LANES].reshape(dims))
    return matrix, advance, vectors, starts


class PlainBuffers:
    def __init__(self):
        self.pieces = {}

    def matrix(self, first, left, right):
        self.pieces[first] = lax.dot_general(
            left, right, (((0,), (0,)), ((), ())), preferred_element_type=F32
        ).reshape(-1)

    def vectors(self, first, rows):
        self.pieces[first] = rows.astype(F32).reshape(-1)


def plain_body(params, moment_one, moment_two, inputs, cotangent, segments, windows):
    opt_count, dp_count = lax.axis_size("opt"), lax.axis_size("dp")
    flat = lax.all_gather(params, "opt", axis=0, tiled=True)
    starts, weights = [0], []
    for dims in layout_of(inputs.shape[2], FF):
        amount = math.prod(dims)
        at = starts[-1] * LANES
        weights.append(flat[at : at + amount].reshape(dims))
        starts.append(starts[-1] + amount // LANES)
    buffers = PlainBuffers()
    output, input_grad = compute(
        lambda n: weights[n],
        lambda n: None,
        weights[4:],
        inputs,
        cotangent,
        segments,
        windows,
        buffers,
        starts,
        Line(),
        lambda k: None,
    )
    total = jnp.concatenate([buffers.pieces[first] for first in sorted(buffers.pieces)])
    blocks = total.reshape(opt_count, dp_count, -1).transpose(1, 0, 2)
    own = lax.psum_scatter(
        blocks.reshape(opt_count * dp_count, -1), ("dp", "opt"), scatter_dimension=0, tiled=True
    )
    grads = lax.all_gather(own, "dp", axis=0, tiled=True).reshape(-1)
    length = params.shape[0]
    position = lax.axis_index("opt") * length + jnp.arange(length, dtype=jnp.int32)
    decay = jnp.where(position < MATRIX_PARAMS, WEIGHT_DECAY, 0.0)
    old = params.astype(F32)
    first = 0.5 * moment_one + 0.5 * grads
    second = 0.5 * moment_two + 0.5 * grads * grads
    new = old - LEARN_RATE * (first / (jnp.sqrt(second) + 1e-08) + decay * old)
    return (output, input_grad, grads, new, first, second, new.astype(BF))


def body(params, moment_one, moment_two, inputs, cotangent, segments, windows):
    opt_count, dp_count = lax.axis_size("opt"), lax.axis_size("dp")
    opt_me, dp_me = lax.axis_index("opt"), lax.axis_index("dp")
    layout = layout_of(inputs.shape[2], FF)
    shard_rows = params.shape[0] // LANES
    if params.shape[0] % (8 * LANES) or opt_count == 1 or dp_count < 4:
        return plain_body(params, moment_one, moment_two, inputs, cotangent, segments, windows)
    state = [v.reshape(shard_rows, LANES) for v in (params, moment_one, moment_two)]
    line, results = Line(), []
    matrix, advance, vectors, starts = gather_weights(
        state[0], layout, opt_count, dp_count, opt_me, dp_me, line
    )
    count, unit, orders = rounds_of(shard_rows, opt_count, dp_count)
    step = dp_count * unit
    buffers = RoundBuffers(line, shard_rows, step, count, opt_count)
    rounds = [
        round_task(k, line, buffers, orders, state, results, unit, opt_me, dp_me, opt_count, dp_count)
        for k in range(count)
    ]

    def turn_of(k):
        if k < count and not buffers.left[k]:
            next(rounds[k], None)

    output, input_grad = compute(
        matrix, advance, vectors, inputs, cotangent, segments, windows, buffers, starts, line, turn_of
    )
    for k in POST_ORDER:
        turn_of(k)
    for task in rounds:
        for _ in task:
            pass
    return (output, input_grad, *[r.reshape(-1) for r in results])


def rounds_of(shard_rows, opt_count, dp_count):
    orders = halving_orders(bits_of(opt_count), bits_of(dp_count))
    for count in range(ROUNDS, 0, -1):
        piece = -(-shard_rows // (count * dp_count * 16)) * 16
        if (count * dp_count - 1) * piece < shard_rows:
            return count, piece, orders
    piece = -(-shard_rows // (dp_count * 8)) * 8
    assert (dp_count - 1) * piece < shard_rows
    return 1, piece, orders[:1]


def round_task(k, line, buffers, orders, state, results, piece, opt_me, dp_me, opt_count, dp_count):
    sums = Halving(line, buffers.arrays[k], orders, dp_count, opt_count)
    for n in range(sums.steps):
        recvs = sums.exchange(n, sums.sums(n))
        yield
        sums.incoming(n, recvs)
    turn = jnp.where(opt_me < opt_count // 2, buffers.rounds - 1 - k, k)
    places = np.array([spread_place(p, dp_count) for p in range(dp_count)])

    def update(grads, part):
        blocks = turn * dp_count + (dp_me ^ places[part])
        done = adam(line, grads, *state, blocks, opt_me * buffers.shard_rows, piece, results)
        results[:] = done

    half = dp_count // 2
    spread = Spread(line, sums.sums(None)[0], dp_count, dp_count)
    while spread.bits:
        last = spread.bits[0] == 0
        recvs = spread.exchange(spread.outgoing())
        if last:
            update(spread.near, slice(0, half))
        yield
        spread.incoming(recvs)
    update(spread.far, slice(half, None))


def solution(mesh):
    placed = (
        P("opt"),
        P("opt"),
        P("opt"),
        P(("dp", "opt"), None, None),
        P(("dp", "opt"), None, None),
        P(("dp", "opt"), None),
        P(("dp", "opt")),
    )
    return jax.shard_map(
        body,
        mesh=mesh,
        in_specs=placed,
        out_specs=(
            P(("dp", "opt"), None, None),
            P(("dp", "opt"), None, None),
            P("opt"),
            P("opt"),
            P("opt"),
            P("opt"),
            P("opt"),
        ),
        check_vma=False,
    )
```
